32 devices in a mesh: rep: 4 (over y, core), shard: 8 (over z, x).
Axes of the slice: x: 2, y: 2, z: 4, core: 2. Of those that a mesh axis runs over, the one named last changes fastest.
Arguments:
- grad_kv: bfloat16 [4, 2, 8192, 1024], P('rep', None, 'shard'), may hold values from -24 to 24
- error_kv: float32 [4, 2, 8192, 1024], P('rep', None, 'shard'), may hold values from -12 to 12
- basis_kv: float32 [2, 1024, 64], replicated, may hold values from -6 to 6
Outputs:
- update_kv: bfloat16 [2, 8192, 1024], P(None, 'shard')
- new_error: float32 [4, 2, 8192, 1024], P('rep', None, 'shard')
- basis_next: float32 [2, 1024, 64], replicated
The draws below stay inside these ranges and needn't reach their ends.
All inputs are finite; a program needn't handle non-finite values.
Results may differ from the reference program's by a relative error of at most 0.001.
Values sent between devices are 32-bit elements; how exact they have to be, the bound alone decides.
No kernel may reach another device: no remote copies, remote signals or barrier semaphores. Data moves between devices by JAX's collectives and lax.ppermute only.
A program may use at most 64 MiB of HBM per device.

```python
import jax
import jax.numpy as jnp
from jax import lax

D = 8192
RANK = 64
KVC = 1024
REPLICAS = 4
N_REP = 4


def block_levels(rng, shape, pieces, least, high):
    gain = 1.0
    for position, shards_of in pieces:
        steps = jax.random.uniform(jax.random.fold_in(jax.random.fold_in(rng, 6), position), (shards_of,), jnp.float32, least / len(pieces), high / len(pieces))
        gain = gain * jnp.repeat(jnp.exp(steps), shape[position] // shards_of).reshape((-1,) + (1,) * (len(shape) - 1 - position))
    return gain


def centred(rng, shape, deviation, bound, cuts=(), kind=jnp.bfloat16):
    loudness = block_levels(rng, shape, cuts, -0.22, 0.18) if cuts else 1.0
    array = jax.random.normal(rng, shape, jnp.float32) * deviation * loudness
    return jnp.minimum(jnp.maximum(array, -bound), bound).astype(kind)


def setup_inputs(seed: int = 0) -> dict:
    keys = jax.random.split(jax.random.key(seed), 4)
    return {
        "grad_kv": centred(keys[0], (REPLICAS, 2, D, KVC), 4.0, 24.0, ((0, 4), (2, 8))),
        "error_kv": centred(keys[1], (REPLICAS, 2, D, KVC), 2.0, 12.0, ((0, 4), (2, 8)), jnp.float32),
        "basis_kv": centred(keys[2], (2, KVC, RANK), 1.0, 6.0, (), jnp.float32),
    }


def reference(grad_kv, error_kv, basis_kv):
    highest = lax.Precision.HIGHEST
    merged = grad_kv.astype(jnp.float32) + error_kv
    left = jnp.einsum('smrc,mck->mrk', merged, basis_kv, precision=highest) / N_REP
    gram = jnp.einsum('mrk,mrl->mkl', left, left, precision=highest)
    chol = jnp.linalg.cholesky(gram)
    ortho = lax.linalg.triangular_solve(chol, left, left_side=False, lower=True, transpose_a=True)
    basis_next = jnp.einsum('smrc,mrk->mck', merged, ortho, precision=highest) / N_REP
    approx = jnp.einsum('mrk,mck->mrc', ortho, basis_next, precision=highest)
    new_error = merged - approx[None]
    return (approx.astype(jnp.bfloat16), new_error, basis_next)
```

```python
import functools

import jax
import jax.numpy as jnp
from jax import lax
from jax.experimental import pallas as pl
from jax.experimental.pallas import tpu as pltpu
from jax.sharding import PartitionSpec as P

AXES = ("rep", "shard")
F32, BF16 = jnp.float32, jnp.bfloat16
HIGHEST = lax.Precision.HIGHEST
NT = (((1,), (1,)), ((), ()))
TN = (((0,), (0,)), ((), ()))
NN = (((1,), (0,)), ((), ()))


def dot(a, b, dims, precision=None):
    return lax.dot_general(a, b, dims, precision=precision, preferred_element_type=F32)


def split(x):
    high = x.astype(BF16)
    return high, (x - high.astype(F32)).astype(BF16)


def params(mib, axes=1):
    return pltpu.CompilerParams(
        vmem_limit_bytes=mib << 20, dimension_semantics=("arbitrary",) * axes
    )


def left_kernel(which, grad, error, basis, high, low, left, cut):
    rank = basis.shape[1]

    @pl.when(pl.program_id(0) == 0)
    def _():
        top, rest = split(basis[0])
        cut[:rank] = top
        cut[rank:] = rest

    merged = grad[0, 0].astype(F32) + error[0, 0]
    top, rest = split(merged)
    high[...] = top
    low[...] = rest
    both = dot(cut[...], top, NT)
    left[...] = both[:rank] + both[rank:] + dot(cut[:rank], rest, NT)


def left_of(which, grad, error, basis):
    _, _, rows, cols = grad.shape
    rank = basis.shape[1]
    block = min(rows, 256)
    tile = pl.BlockSpec((1, 1, block, cols), lambda i, w: (0, w[0], i, 0))
    flat = pl.BlockSpec((block, cols), lambda i, w: (i, 0))
    return pl.pallas_call(
        left_kernel,
        name="left",
        grid_spec=pltpu.PrefetchScalarGridSpec(
            num_scalar_prefetch=1,
            grid=(rows // block,),
            in_specs=[tile, tile, pl.BlockSpec((1, rank, cols), lambda i, w: (w[0], 0, 0))],
            out_specs=[flat, flat, pl.BlockSpec((rank, block), lambda i, w: (0, i))],
            scratch_shapes=[pltpu.VMEM((2 * rank, cols), BF16)],
        ),
        out_shape=[
            jax.ShapeDtypeStruct((rows, cols), BF16),
            jax.ShapeDtypeStruct((rows, cols), BF16),
            jax.ShapeDtypeStruct((rank, rows), F32),
        ],
        compiler_params=params(24),
        cost_estimate=pl.CostEstimate(
            flops=6 * rows * cols * rank, bytes_accessed=10 * rows * cols, transcendentals=0
        ),
    )(which, grad, error, basis)


def right_kernel(left, high, low, right):
    rank = left.shape[0]
    top, rest = split(left[...])
    both = dot(jnp.concatenate([top, rest], axis=0), high[...], NN)
    right[...] = both[:rank] + both[rank:] + dot(top, low[...], NN)


def right_of(left, high, low, part, parts):
    rows, cols = high.shape
    rank = left.shape[0]
    width = cols // parts
    block = min(width, 256)
    steps = width // block
    tile = pl.BlockSpec((rows, block), lambda i: (0, part * steps + i))
    return pl.pallas_call(
        right_kernel,
        name="right",
        grid=(steps,),
        in_specs=[pl.BlockSpec((rank, rows), lambda i: (0, 0)), tile, tile],
        out_specs=pl.BlockSpec((rank, block), lambda i: (0, i)),
        out_shape=jax.ShapeDtypeStruct((rank, width), F32),
        compiler_params=params(24),
        cost_estimate=pl.CostEstimate(
            flops=6 * rows * width * rank, bytes_accessed=4 * rows * width, transcendentals=0
        ),
    )(left, high, low)


def gram_kernel(scale, mine, theirs, left, gram):
    left[...] = (mine[...] + theirs[...]) * scale
    gram[...] = dot(left[...], left[...], NT, HIGHEST)


def gram_of(mine, theirs, scale):
    rank, rows = mine.shape
    return pl.pallas_call(
        functools.partial(gram_kernel, scale),
        name="gram",
        out_shape=[
            jax.ShapeDtypeStruct((rank, rows), F32),
            jax.ShapeDtypeStruct((rank, rank), F32),
        ],
        compiler_params=params(8, 0),
        cost_estimate=pl.CostEstimate(
            flops=12 * rank * rank * rows, bytes_accessed=12 * rank * rows, transcendentals=0
        ),
    )(mine, theirs)


def factor_kernel(gram, theirs, inverse):
    rank = gram.shape[0]
    row = lax.broadcasted_iota(jnp.int32, (rank, rank), 0)
    col = lax.broadcasted_iota(jnp.int32, (rank, rank), 1)
    eye = jnp.where(row == col, 1.0, 0.0)
    work = jnp.concatenate([gram[...] + theirs[...], eye], axis=1)
    below = lax.broadcasted_iota(jnp.int32, (rank, 1), 0)
    for j in range(rank - 1):
        pivot = work[j : j + 1, :]
        scaled = pivot * (1.0 / work[j : j + 1, j : j + 1])
        factor = jnp.where(below > j, work[:, j : j + 1], 0.0)
        work = work - factor * scaled
    diagonal = jnp.sum(work[:, :rank] * eye, axis=1, keepdims=True)
    inverse[...] = work[:, rank:] / jnp.sqrt(diagonal)


def factor_of(gram, theirs):
    rank = gram.shape[0]
    return pl.pallas_call(
        factor_kernel,
        name="factor",
        out_shape=jax.ShapeDtypeStruct((rank, rank), F32),
        compiler_params=params(8, 0),
        cost_estimate=pl.CostEstimate(
            flops=4 * rank**3, bytes_accessed=12 * rank * rank, transcendentals=rank
        ),
    )(gram, theirs)


def apply_kernel(scale, inverse, mine, theirs, out):
    out[...] = dot(inverse[...], (mine[...] + theirs[...]) * scale, NN, HIGHEST)


def apply_of(inverse, mine, theirs, scale):
    return pl.pallas_call(
        functools.partial(apply_kernel, scale),
        name="apply",
        out_shape=jax.ShapeDtypeStruct(mine.shape, F32),
        compiler_params=params(8, 0),
    )(inverse, mine, theirs)


def final_kernel(which, inverse, left, right, high, low, *refs):
    update, new_error, basis_next, ortho = refs[-4:]
    rank = left.shape[0]

    @pl.when(pl.program_id(0) == 0)
    def _():
        top, rest = split(dot(inverse[...], left[...], NN, HIGHEST))
        ortho[:rank] = top
        ortho[rank : 2 * rank] = top
        ortho[2 * rank :] = rest

    top, rest = split(right[...])
    approx = dot(ortho[...], jnp.concatenate([top, rest, top], axis=0), TN)
    update[0] = approx.astype(BF16)
    new_error[0, 0] = (high[...].astype(F32) + low[...].astype(F32)) - approx
    basis_next[0] = right[...]


def final_of(which, inverse, left, right, high, low, outs, part, parts):
    rows, cols = high.shape
    rank = left.shape[0]
    width = cols // parts
    block = min(width, 256)
    steps = width // block
    tile = pl.BlockSpec((rows, block), lambda i, w: (0, part * steps + i))
    whole = lambda shape: pl.BlockSpec(shape, lambda i, w: (0, 0))
    return pl.pallas_call(
        final_kernel,
        name="final",
        grid_spec=pltpu.PrefetchScalarGridSpec(
            num_scalar_prefetch=1,
            grid=(steps,),
            in_specs=[
                whole((rank, rank)),
                whole((rank, rows)),
                pl.BlockSpec((rank, block), lambda i, w: (0, i)),
                tile,
                tile,
            ]
            + [pl.BlockSpec(memory_space=pl.ANY)] * len(outs),
            out_specs=[
                pl.BlockSpec((1, rows, block), lambda i, w: (w[0], 0, part * steps + i)),
                pl.BlockSpec((1, 1, rows, block), lambda i, w: (0, w[0], 0, part * steps + i)),
                pl.BlockSpec((1, rank, block), lambda i, w: (w[0], 0, part * steps + i)),
            ],
            scratch_shapes=[pltpu.VMEM((3 * rank, rows), BF16)],
        ),
        out_shape=[
            jax.ShapeDtypeStruct((2, rows, cols), BF16),
            jax.ShapeDtypeStruct((1, 2, rows, cols), F32),
            jax.ShapeDtypeStruct((2, rank, cols), F32),
        ],
        input_output_aliases={6 + k: k for k in range(len(outs))},
        compiler_params=params(32),
        cost_estimate=pl.CostEstimate(
            flops=6 * rows * width * rank, bytes_accessed=10 * rows * width, transcendentals=0
        ),
    )(which, inverse, left, right, high, low, *outs)


def bits_of(count):
    return [1 << k for k in range(count.bit_length() - 1)]


def on_device(replicas, shards, grad_kv, error_kv, basis_kv):
    def swap(value, rep_mask, shard_mask):
        pairs = [
            (r * shards + s, (r ^ rep_mask) * shards + (s ^ shard_mask))
            for r in range(replicas)
            for s in range(shards)
        ]
        return lax.ppermute(value, AXES, pairs)

    core = functools.partial(swap, rep_mask=1, shard_mask=0)
    rep_steps = [(mask, 0) for mask in bits_of(replicas)[1:]]
    masks = bits_of(shards)
    masks[-1] |= masks[-2]
    shard_steps = [(0, mask) for mask in masks]
    scale = 1.0 / replicas

    basis = basis_kv.transpose(0, 2, 1)
    mine = (lax.axis_index("rep") % 2).astype(jnp.int32).reshape(1)
    theirs = 1 - mine

    high_t, low_t, left_t = left_of(theirs, grad_kv, error_kv, basis)
    arriving = core(left_t)
    high_m, low_m, left_m = left_of(mine, grad_kv, error_kv, basis)
    left_m = left_m + arriving
    for step in rep_steps[:-1]:
        left_m = left_m + swap(left_m, *step)
    left_m, gram = gram_of(left_m, swap(left_m, *rep_steps[-1]), scale)
    left_t = core(left_m)

    for step in shard_steps[:-1]:
        gram = gram + swap(gram, *step)
    inverse_m = factor_of(gram, swap(gram, *shard_steps[-1]))
    inverse_t = core(inverse_m)

    orders = (rep_steps + shard_steps, shard_steps[:1] + rep_steps + shard_steps[:0:-1])
    parts = len(orders)
    rights = []
    for part, order in enumerate(orders):
        right_t = core(right_of(left_t, high_t, low_t, part, parts))
        right = right_of(left_m, high_m, low_m, part, parts) + right_t
        for step in order[:-1]:
            right = right + swap(right, *step)
        right_m = apply_of(inverse_m, right, swap(right, *order[-1]), scale)
        rights.append((right_m, core(right_m)))

    outs = ()
    for part, (right_m, right_t) in enumerate(rights):
        outs = final_of(mine, inverse_m, left_m, right_m, high_m, low_m, outs, part, parts)
        outs = final_of(theirs, inverse_t, left_t, right_t, high_t, low_t, outs, part, parts)
    update, new_error, right = outs
    return update, new_error, right.transpose(0, 2, 1)


def solution(mesh):
    placed = (P("rep", None, "shard", None), P("rep", None, "shard", None), P())
    return jax.shard_map(
        functools.partial(on_device, mesh.shape["rep"], mesh.shape["shard"]),
        mesh=mesh,
        in_specs=placed,
        out_specs=(P(None, "shard", None), P("rep", None, "shard", None), P()),
        check_vma=False,
    )
```

```python
import functools

import jax
import jax.numpy as jnp
from jax import lax
from jax.experimental import pallas as pl
from jax.experimental.pallas import tpu as pltpu
from jax.sharding import PartitionSpec as P

AXES = ("rep", "shard")
F32, BF16 = jnp.float32, jnp.bfloat16
HIGHEST = lax.Precision.HIGHEST
NT = (((1,), (1,)), ((), ()))
TN = (((0,), (0,)), ((), ()))
NN = (((1,), (0,)), ((), ()))
LANES = 128
VMEM = pl.BlockSpec(memory_space=pltpu.VMEM)


def dot(a, b, dims, precision=None):
    return lax.dot_general(a, b, dims, precision=precision, preferred_element_type=F32)


def split(x):
    high = x.astype(BF16)
    return high, (x - high.astype(F32)).astype(BF16)


def params(mib, axes=1):
    return pltpu.CompilerParams(
        vmem_limit_bytes=mib << 20, dimension_semantics=("arbitrary",) * axes
    )


def left_kernel(which, grad, error, basis, high, low, left, cut):
    rank = basis.shape[1]

    @pl.when(pl.program_id(0) == 0)
    def _():
        top, rest = split(basis[0])
        cut[:rank] = top
        cut[rank:] = rest

    merged = grad[0, 0].astype(F32) + error[0, 0]
    top, rest = split(merged)
    high[...] = top
    low[...] = rest
    both = dot(cut[...], top, NT)
    left[...] = both[:rank] + both[rank:] + dot(cut[:rank], rest, NT)


def left_of(which, grad, error, basis):
    _, _, rows, cols = grad.shape
    rank = basis.shape[1]
    block = min(rows, 256)
    tile = pl.BlockSpec((1, 1, block, cols), lambda i, w: (0, w[0], i, 0))
    flat = pl.BlockSpec((block, cols), lambda i, w: (i, 0))
    return pl.pallas_call(
        left_kernel,
        name="left",
        grid_spec=pltpu.PrefetchScalarGridSpec(
            num_scalar_prefetch=1,
            grid=(rows // block,),
            in_specs=[tile, tile, pl.BlockSpec((1, rank, cols), lambda i, w: (w[0], 0, 0))],
            out_specs=[flat, flat, pl.BlockSpec((rank, block), lambda i, w: (0, i))],
            scratch_shapes=[pltpu.VMEM((2 * rank, cols), BF16)],
        ),
        out_shape=[
            jax.ShapeDtypeStruct((rows, cols), BF16),
            jax.ShapeDtypeStruct((rows, cols), BF16),
            jax.ShapeDtypeStruct((rank, rows), F32),
        ],
        compiler_params=params(24),
        cost_estimate=pl.CostEstimate(
            flops=6 * rows * cols * rank, bytes_accessed=10 * rows * cols, transcendentals=0
        ),
    )(which, grad, error, basis)


def right_kernel(start, with_gram, left, high, low, right):
    rank = left.shape[0]
    width = right.shape[1] - (LANES if with_gram else 0)
    top, rest = split(left[...])
    columns = slice(start, start + width)
    both = dot(jnp.concatenate([top, rest], axis=0), high[:, columns], NN)
    right[:, :width] = both[:rank] + both[rank:] + dot(top, low[:, columns], NN)
    if with_gram:
        right[:, width:] = jnp.zeros((rank, LANES), F32)
        right[:, width : width + rank] = dot(left[...], left[...], NT, HIGHEST)


def right_of(left, high, low, start, width, with_gram=False):
    rows, cols = high.shape
    rank = left.shape[0]
    return pl.pallas_call(
        functools.partial(right_kernel, start, with_gram),
        name="right",
        in_specs=[VMEM] * 3,
        out_specs=VMEM,
        out_shape=jax.ShapeDtypeStruct((rank, width + (LANES if with_gram else 0)), F32),
        compiler_params=params(16, 0),
        cost_estimate=pl.CostEstimate(
            flops=6 * rows * width * rank, bytes_accessed=4 * rows * width, transcendentals=0
        ),
    )(left, high, low)


def factor_kernel(scale, right_scale, mine, theirs, inverse, right):
    rank = mine.shape[0]
    width = right.shape[1]
    row = lax.broadcasted_iota(jnp.int32, (rank, rank), 0)
    col = lax.broadcasted_iota(jnp.int32, (rank, rank), 1)
    eye = jnp.where(row == col, 1.0, 0.0)
    columns = slice(width, width + rank)
    gram = (mine[:, columns] + theirs[:, columns]) * scale
    work = jnp.concatenate([gram, eye], axis=1)
    below = lax.broadcasted_iota(jnp.int32, (rank, 1), 0)
    for j in range(rank - 1):
        pivot = work[j : j + 1, :]
        scaled = pivot * (1.0 / work[j : j + 1, j : j + 1])
        factor = jnp.where(below > j, work[:, j : j + 1], 0.0)
        work = work - factor * scaled
    diagonal = jnp.sum(work[:, :rank] * eye, axis=1, keepdims=True)
    inverse[...] = work[:, rank:] / jnp.sqrt(diagonal)
    total = (mine[:, :width] + theirs[:, :width]) * right_scale
    right[...] = dot(inverse[...], total, NN, HIGHEST)


def factor_of(mine, theirs, scale, right_scale):
    rank = mine.shape[0]
    width = mine.shape[1] - LANES
    return pl.pallas_call(
        functools.partial(factor_kernel, scale, right_scale),
        name="factor",
        in_specs=[VMEM] * 2,
        out_specs=[VMEM] * 2,
        out_shape=[
            jax.ShapeDtypeStruct((rank, rank), F32),
            jax.ShapeDtypeStruct((rank, width), F32),
        ],
        compiler_params=params(8, 0),
        cost_estimate=pl.CostEstimate(
            flops=4 * rank**3, bytes_accessed=8 * rank * width, transcendentals=rank
        ),
    )(mine, theirs)


def apply_kernel(scale, inverse, mine, theirs, out):
    out[...] = dot(inverse[...], (mine[...] + theirs[...]) * scale, NN, HIGHEST)


def apply_of(inverse, mine, theirs, scale):
    return pl.pallas_call(
        functools.partial(apply_kernel, scale),
        name="apply",
        in_specs=[VMEM] * 3,
        out_specs=VMEM,
        out_shape=jax.ShapeDtypeStruct(mine.shape, F32),
        compiler_params=params(8, 0),
    )(inverse, mine, theirs)


def final_kernel(counts, which, inverse, left, high, low, *refs):
    rights, (update, new_error, basis_next, ortho, pieces) = refs[:counts], refs[-5:]
    rank = left.shape[0]

    @pl.when(pl.program_id(0) == 0)
    def _():
        top, rest = split(dot(left[...], inverse[...], (((0,), (1,)), ((), ())), HIGHEST))
        ortho[:, :rank] = top
        ortho[:, rank : 2 * rank] = top
        ortho[:, 2 * rank :] = rest
        start = 0
        for right in rights:
            columns = slice(start, start + right.shape[1])
            top, rest = split(right[...])
            pieces[:rank, columns] = top
            pieces[rank : 2 * rank, columns] = rest
            pieces[2 * rank :, columns] = top
            basis_next[0, :, columns] = right[...]
            start += right.shape[1]

    block = high.shape[0]
    rows = pl.ds(pl.multiple_of(pl.program_id(0) * block, block), block)
    approx = dot(ortho[rows, :], pieces[...], NN)
    update[0] = approx.astype(BF16)
    new_error[0, 0] = (high[...].astype(F32) + low[...].astype(F32)) - approx


def final_of(which, inverse, left, high, low, rights, outs):
    rows, cols = high.shape
    rank = left.shape[0]
    block = min(rows, 128)
    tile = pl.BlockSpec((block, cols), lambda i, w: (i, 0))
    whole = lambda shape: pl.BlockSpec(shape, lambda i, w: (0, 0))
    return pl.pallas_call(
        functools.partial(final_kernel, len(rights)),
        name="final",
        grid_spec=pltpu.PrefetchScalarGridSpec(
            num_scalar_prefetch=1,
            grid=(rows // block,),
            in_specs=[whole((rank, rank)), whole((rank, rows)), tile, tile]
            + [whole(right.shape) for right in rights]
            + [pl.BlockSpec(memory_space=pl.ANY)] * len(outs),
            out_specs=[
                pl.BlockSpec((1, block, cols), lambda i, w: (w[0], i, 0)),
                pl.BlockSpec((1, 1, block, cols), lambda i, w: (0, w[0], i, 0)),
                pl.BlockSpec((1, rank, cols), lambda i, w: (w[0], 0, 0)),
            ],
            scratch_shapes=[pltpu.VMEM((rows, 3 * rank), BF16), pltpu.VMEM((3 * rank, cols), BF16)],
        ),
        out_shape=[
            jax.ShapeDtypeStruct((2, rows, cols), BF16),
            jax.ShapeDtypeStruct((1, 2, rows, cols), F32),
            jax.ShapeDtypeStruct((2, rank, cols), F32),
        ],
        input_output_aliases={5 + len(rights) + k: k for k in range(len(outs))},
        compiler_params=params(16),
        cost_estimate=pl.CostEstimate(
            flops=6 * rows * cols * rank, bytes_accessed=10 * rows * cols, transcendentals=0
        ),
    )(which, inverse, left, high, low, *rights, *outs)


def bits_of(count):
    return [1 << k for k in range(count.bit_length() - 1)]


def on_device(replicas, shards, grad_kv, error_kv, basis_kv):
    def swap(value, *masks):
        pairs = []
        for r in range(replicas):
            for s in range(shards):
                rep_mask, shard_mask = masks[r % len(masks)]
                pairs.append((r * shards + s, (r ^ rep_mask) * shards + (s ^ shard_mask)))
        return lax.ppermute(value, AXES, pairs)

    def core(value):
        return swap(value, (1, 0))

    rep_steps = [(mask, 0) for mask in bits_of(replicas)[1:]]
    masks = bits_of(shards)
    masks[-1] |= masks[-2]
    steps = rep_steps + [(0, mask) for mask in masks]
    scale = 1.0 / replicas

    def order(part):
        turns = [steps[turn:] + steps[:turn] for turn in (2 * part, 2 * part + 1)]
        return list(zip(*turns))

    grad_kv, error_kv = (pltpu.with_memory_space_constraint(x, pltpu.HBM) for x in (grad_kv, error_kv))
    basis = basis_kv.transpose(0, 2, 1)
    mine = (lax.axis_index("rep") % 2).astype(jnp.int32).reshape(1)
    theirs = 1 - mine

    high_t, low_t, left_t = left_of(theirs, grad_kv, error_kv, basis)
    arriving = core(left_t)
    high_m, low_m, left_m = left_of(mine, grad_kv, error_kv, basis)
    left_m = left_m + arriving
    for step in rep_steps:
        left_m = left_m + swap(left_m, step)
    left_m = left_m * scale
    left_t = core(left_m)

    cols = high_m.shape[1]
    first = cols * 3 // 8
    pieces = ((0, first), (first, cols - first))
    sums = []
    for part, (start, width) in enumerate(pieces):
        right_t = core(right_of(left_t, high_t, low_t, start, width))
        right = right_of(left_m, high_m, low_m, start, width, part == 0)
        right = right + jnp.pad(right_t, ((0, 0), (0, right.shape[1] - width)))
        *early, last = order(part)
        for step in early:
            right = right + swap(right, *step)
        sums.append((right, swap(right, *last)))

    inverse_m, right_a = factor_of(*sums[0], 2.0 / replicas, scale)
    right_b = apply_of(inverse_m, *sums[1], scale)
    rights_m = (right_a, right_b)
    inverse_t = core(inverse_m)
    rights_t = tuple(core(right) for right in rights_m)

    outs = final_of(mine, inverse_m, left_m, high_m, low_m, rights_m, ())
    outs = final_of(theirs, inverse_t, left_t, high_t, low_t, rights_t, outs)
    update, new_error, right = outs
    return update, new_error, right.transpose(0, 2, 1)


def solution(mesh):
    placed = (P("rep", None, "shard", None), P("rep", None, "shard", None), P())
    return jax.shard_map(
        functools.partial(on_device, mesh.shape["rep"], mesh.shape["shard"]),
        mesh=mesh,
        in_specs=placed,
        out_specs=(P(None, "shard", None), P("rep", None, "shard", None), P()),
        check_vma=False,
    )
```

```python
import functools

import jax
import jax.numpy as jnp
from jax import lax
from jax.experimental import pallas as pl
from jax.experimental.pallas import tpu as pltpu
from jax.sharding import PartitionSpec as P


AXES = ("rep", "shard")
DEPTH = 4
LEFT_ROWS = 256
FINAL_ROWS = 128
F32, BF16 = jnp.float32, jnp.bfloat16
HIGHEST = lax.Precision.HIGHEST
NT = (((1,), (1,)), ((), ()))
NN = (((1,), (0,)), ((), ()))
TT = (((0,), (1,)), ((), ()))
VMEM = pl.BlockSpec(memory_space=pltpu.VMEM)
SMEM = pl.BlockSpec(memory_space=pltpu.SMEM)
ANY = pl.BlockSpec(memory_space=pl.ANY)


def dot(a, b, dims, precision=None):
    return lax.dot_general(a, b, dims, precision=precision, preferred_element_type=F32)


def split(x):
    high = x.astype(BF16)
    return high, (x - high.astype(F32)).astype(BF16)


def params(mib):
    return pltpu.CompilerParams(vmem_limit_bytes=mib << 20)


def bit(code, index):
    return (code[0] >> index) & 1


def shape_of(*shape, dtype=F32):
    return jax.ShapeDtypeStruct(shape, dtype)


def left_kernel(block, jobs, code, grad, error, basis, *refs):
    outs, (grads, errors, factors, sems) = refs[-4 - 3 * len(jobs) : -4], refs[-4:]
    rank = basis.shape[1]
    copies = [pltpu.make_async_copy(basis, factors, sems.at[2, 0])]
    copies[0].start()
    blocks = []
    for job, (which, begin, end) in enumerate(jobs):
        w = bit(code, which)
        for start in range(begin, end, block):
            i = len(blocks)
            source, target = pl.ds(start, block), pl.ds(i * block, block)
            pair = (
                pltpu.make_async_copy(error.at[0, w, source], errors.at[target], sems.at[0, i]),
                pltpu.make_async_copy(grad.at[0, w, source], grads.at[target], sems.at[1, i]),
            )
            blocks.append((job, start, pair))

    def begin_block(i):
        if i < len(blocks):
            for copy in blocks[i][2]:
                copy.start()

    for i in range(DEPTH):
        begin_block(i)
    copies[0].wait()
    cuts = []
    for which, _, _ in jobs:
        top, rest = split(factors[bit(code, which)])
        cuts.append((top, jnp.concatenate([top, rest], axis=0)))
    for i, (job, start, pair) in enumerate(blocks):
        for copy in pair:
            copy.wait()
        begin_block(i + DEPTH)
        top, cut = cuts[job]
        high, low, left = outs[3 * job : 3 * job + 3]
        source, target = slice(start, start + block), slice(i * block, (i + 1) * block)
        upper, lower = split(grads[target].astype(F32) + errors[target])
        high[source] = upper
        low[source] = lower
        both = dot(cut, upper, NT)
        left[:, source] = both[:rank] + both[rank:] + dot(top, lower, NT)


def left_of(jobs, code, grad, error, basis, before=()):
    _, _, rows, cols = grad.shape
    rank = basis.shape[1]
    block = min(rows // 2, LEFT_ROWS)
    total = sum(end - begin for _, begin, end in jobs)
    return pl.pallas_call(
        functools.partial(left_kernel, block, jobs),
        name="left",
        in_specs=[SMEM, ANY, ANY, ANY] + [VMEM] * len(before),
        out_specs=[VMEM] * (3 * len(jobs)),
        out_shape=[
            shape_of(rows, cols, dtype=BF16),
            shape_of(rows, cols, dtype=BF16),
            shape_of(rank, rows),
        ]
        * len(jobs),
        scratch_shapes=[
            pltpu.VMEM((total, cols), BF16),
            pltpu.VMEM((total, cols), F32),
            pltpu.VMEM(basis.shape, F32),
            pltpu.SemaphoreType.DMA((3, total // block)),
        ],
        input_output_aliases={4 + k: k for k in range(len(before))},
        compiler_params=params(16),
        cost_estimate=pl.CostEstimate(
            flops=6 * total * cols * rank, bytes_accessed=10 * total * cols, transcendentals=0
        ),
    )(code, grad, error, basis, *before)


def ordered(left, keep):
    half = left.shape[0] // 2
    pick = lambda index: left[pl.ds(pl.multiple_of(index * half, half), half), :]
    return jnp.concatenate([pick(1 - keep), pick(keep)], axis=0)


def product(left, high, low, columns):
    rank = left.shape[0]
    top, rest = split(left)
    both = dot(jnp.concatenate([top, rest], axis=0), high[:, columns], NN)
    return both[:rank] + both[rank:] + dot(top, low[:, columns], NN)


def right_kernel(starts, keeps, with_gram, code, left, high, low, *outs):
    for start, keep, right in zip(starts, keeps, outs):
        columns = slice(start, start + right.shape[1])
        chosen = left[...] if keep is None else ordered(left, bit(code, keep))
        right[...] = product(chosen, high, low, columns)
    if with_gram:
        half = left.shape[0] // 2
        gram = dot(left[...], left[...], NT, HIGHEST)
        outs[-1][...] = jnp.concatenate([gram[:half], gram[half:]], axis=1)


def right_of(columns, keeps, code, left, high, low, with_gram=False):
    rows, _ = high.shape
    rank = left.shape[0]
    width = sum(width for _, width in columns)
    out_shape = [shape_of(rank, width) for _, width in columns]
    if with_gram:
        out_shape.append(shape_of(rank // 2, 2 * rank))
    return pl.pallas_call(
        functools.partial(right_kernel, [start for start, _ in columns], keeps, with_gram),
        name="right",
        in_specs=[SMEM] + [VMEM] * 3,
        out_specs=[VMEM] * len(out_shape),
        out_shape=out_shape,
        compiler_params=params(8),
        cost_estimate=pl.CostEstimate(
            flops=6 * rows * width * rank, bytes_accessed=4 * rows * width, transcendentals=0
        ),
    )(code, left, high, low)


def eliminate(whole, begin, end):
    rank = whole.shape[0]
    tile = 8
    work = [whole[i : i + tile] for i in range(0, rank, tile)]
    inside = lax.broadcasted_iota(jnp.int32, (tile, 1), 0)
    spread = lambda array: jnp.broadcast_to(array, (tile, 2 * rank))
    for j in range(begin, end, 2):
        home, at = divmod(j, tile)
        first, second = spread(work[home][at : at + 1]), spread(work[home][at + 1 : at + 2])
        a, b = spread(first[:, j : j + 1]), spread(first[:, j + 1 : j + 2])
        c = spread(second[:, j + 1 : j + 2])
        over = 1.0 / (a * c - b * b)
        one = (c * first - b * second) * over
        two = (a * second - b * first) * over
        for k in range(home, rank // tile):
            x, y = spread(work[k][:, j : j + 1]), spread(work[k][:, j + 1 : j + 2])
            if k == home:
                x = jnp.where(inside > at + 1, x, 0.0)
                y = jnp.where(inside > at + 1, y, 0.0)
            work[k] = work[k] - x * one - y * two
    return jnp.concatenate(work, axis=0)


def opening_kernel(end, packed, out):
    rank = out.shape[0]
    sums = packed[:, packed.shape[1] - 2 * rank :]
    row = lax.broadcasted_iota(jnp.int32, (rank, rank), 0)
    col = lax.broadcasted_iota(jnp.int32, (rank, rank), 1)
    gram = jnp.concatenate([sums[:, :rank], sums[:, rank:]], axis=0)
    whole = jnp.concatenate([gram, jnp.where(row == col, 1.0, 0.0)], axis=1)
    out[...] = eliminate(whole, 0, end)


def closing_kernel(begin, work, inverse):
    rank = inverse.shape[0]
    row = lax.broadcasted_iota(jnp.int32, (rank, 2 * rank), 0)
    col = lax.broadcasted_iota(jnp.int32, (rank, 2 * rank), 1)
    whole = eliminate(work[...], begin, rank - 2)
    above = jnp.concatenate([whole[-1:], whole[:-1]], axis=0)
    before = col == row - 1
    pick = lambda array, mask: jnp.sum(jnp.where(mask, array, 0.0), axis=1, keepdims=True)
    odd = row[:, :1] % 2 == 1
    pivot = jnp.where(odd, pick(above, before), 1.0)
    ratio = jnp.where(odd, pick(whole, before) / pivot, 0.0)
    whole = whole - ratio * above
    inverse[...] = whole[:, rank:] / jnp.sqrt(pick(whole, col == row))


def factor_of(kernel, array, rank, width):
    return pl.pallas_call(
        kernel,
        name="factor",
        in_specs=[VMEM],
        out_specs=VMEM,
        out_shape=shape_of(rank, width),
        compiler_params=params(8),
        cost_estimate=pl.CostEstimate(
            flops=2 * rank**3, bytes_accessed=8 * rank * rank, transcendentals=rank
        ),
    )(array)


def final_kernel(block, scale, keeps, code, *refs):
    update, new_error, basis_next, updates, errors, rights, sems = refs[-7:]
    count = (len(refs) - 7) // 2
    copies = []
    for which in range(2):
        inverse, left, high, low, *totals = refs[count * which : count * (which + 1)]
        rows = left.shape[1]
        w = bit(code, which)
        start = 0
        pieces = []
        for keep, total in zip(keeps, totals):
            columns = slice(start, start + total.shape[1])
            right = dot(inverse[...], ordered(total, 1 - bit(code, keep)) * scale, NN, HIGHEST)
            rights[which, :, columns] = right
            top, rest = split(right)
            pieces.append(jnp.concatenate([top, rest, top], axis=0))
            start += total.shape[1]
        pieces = jnp.concatenate(pieces, axis=1)
        copies.append(pltpu.make_async_copy(rights.at[which], basis_next.at[w], sems.at[which, 2, 0]))
        copies[-1].start()
        top, rest = split(dot(left[...], inverse[...], TT, HIGHEST))
        ortho = jnp.concatenate([top, top, rest], axis=1)
        for i, start in enumerate(range(0, rows, block)):
            part, where = slice(start, start + block), pl.ds(start, block)
            approx = dot(ortho[part], pieces, NN)
            updates[which, part] = approx.astype(BF16)
            errors[which, part] = (high[part].astype(F32) + low[part].astype(F32)) - approx
            for kind, source, target in (
                (0, errors.at[which, where], new_error.at[0, w, where]),
                (1, updates.at[which, where], update.at[w, where]),
            ):
                copies.append(pltpu.make_async_copy(source, target, sems.at[which, kind, i]))
                copies[-1].start()
    for copy in copies:
        copy.wait()


def final_of(keeps, code, mine, theirs, scale):
    rank, rows = mine[1].shape
    cols = mine[2].shape[1]
    block = min(rows, FINAL_ROWS)
    return pl.pallas_call(
        functools.partial(final_kernel, block, scale, keeps),
        name="final",
        in_specs=[SMEM] + [VMEM] * (2 * len(mine)),
        out_specs=[ANY] * 3,
        out_shape=[
            shape_of(2, rows, cols, dtype=BF16),
            shape_of(1, 2, rows, cols),
            shape_of(2, rank, cols),
        ],
        scratch_shapes=[
            pltpu.VMEM((2, rows, cols), BF16),
            pltpu.VMEM((2, rows, cols), F32),
            pltpu.VMEM((2, rank, cols), F32),
            pltpu.SemaphoreType.DMA((2, 3, rows // block)),
        ],
        compiler_params=params(24),
        cost_estimate=pl.CostEstimate(
            flops=12 * rows * cols * rank, bytes_accessed=20 * rows * cols, transcendentals=0
        ),
    )(code, *mine, *theirs)


def bits_of(count):
    return [1 << k for k in range(count.bit_length() - 1)]


def plan(replicas, shards):
    r = [(mask, 0) for mask in bits_of(replicas)[1:]]
    t = [(0, mask) for mask in bits_of(shards)]
    orders = (t + r, r + t)
    return r, t, orders


def on_device(replicas, shards, grad_kv, error_kv, basis_kv):
    def swap(value, masks):
        pairs = [
            (i * shards + j, (i ^ masks[0]) * shards + (j ^ masks[1]))
            for i in range(replicas)
            for j in range(shards)
        ]
        return lax.ppermute(value, AXES, pairs)

    def core(value):
        return swap(value, (1, 0))

    r, t, orders = plan(replicas, shards)
    scale = 1.0 / replicas

    rep, shard = lax.axis_index("rep"), lax.axis_index("shard")
    side = rep & 1
    code = side + 2 * (1 - side)
    for part, order in enumerate(orders):
        kept = ((rep & order[0][0]) + (shard & order[0][1]) > 0).astype(jnp.int32)
        code += kept << (2 + part)
    code = code.astype(jnp.int32).reshape(1)
    mine, theirs = 0, 1
    keeps = (2, 3)

    basis = basis_kv.transpose(0, 2, 1)
    grad_kv, error_kv, basis = (
        pltpu.with_memory_space_constraint(x, pltpu.HBM) for x in (grad_kv, error_kv, basis)
    )
    rank = basis.shape[1]
    rows, cols = grad_kv.shape[2:]

    ahead = rows // 2
    jobs = ((theirs, 0, rows), (mine, 0, ahead)), ((mine, ahead, rows),)
    high_t, low_t, left_t, *begun = left_of(jobs[0], code, grad_kv, error_kv, basis)
    arriving = core(left_t)
    high_m, low_m, left_m = left_of(jobs[1], code, grad_kv, error_kv, basis, begun)
    left_m = left_m + arriving
    for step in r:
        left_m = left_m + swap(left_m, step)
    left_m = left_m * scale
    left_t = core(left_m)

    first = cols * 3 // 8
    columns = ((0, first), (first, cols - first))
    *rights, gram = right_of(columns, keeps, code, left_m, high_m, low_m, True)
    arrivals = [
        core(right_of((columns[part],), (keeps[part],), code, left_t, high_t, low_t)[0])
        for part in range(2)
    ]
    totals_m, totals_t = [], []
    for part, (_, width) in enumerate(columns):
        right = rights[part] + arrivals[part]
        send, stay = right[: rank // 2], right[rank // 2 :]
        if part == 0:
            send, stay = (jnp.concatenate([x, gram], axis=1) for x in (send, stay))
        steps = orders[part]
        for turn, step in enumerate(steps):
            if part == 0 and turn == len(t):
                work = factor_of(functools.partial(opening_kernel, rank // 2), stay, rank, 2 * rank)
                inverse_m = factor_of(functools.partial(closing_kernel, rank // 2), work, rank, rank)
                stay = stay[:, :width]
            arrived = swap(send if turn == 0 else stay, step)
            stay = stay + arrived
        back = swap(stay, steps[0])
        total = jnp.concatenate([stay, back], axis=0)
        totals_m.append(total)
        totals_t.append(core(total))
    inverse_t = core(inverse_m)

    update, new_error, right = final_of(
        keeps,
        code,
        (inverse_m, left_m, high_m, low_m, *totals_m),
        (inverse_t, left_t, high_t, low_t, *totals_t),
        scale,
    )
    return update, new_error, right.transpose(0, 2, 1)


def solution(mesh):
    replicas, shards = mesh.shape["rep"], mesh.shape["shard"]
    placed = (P("rep", None, "shard", None), P("rep", None, "shard", None), P())

    def body(*args):
        return on_device(replicas, shards, *args)

    step = jax.shard_map(
        body,
        mesh=mesh,
        in_specs=placed,
        out_specs=(P(None, "shard", None), P("rep", None, "shard", None), P()),
        check_vma=False,
    )
    _, _, _ = plan(replicas, shards)
    return step
```

```python
import functools

import jax
import jax.numpy as jnp
from jax import lax
from jax.experimental import pallas as pl
from jax.experimental.pallas import tpu as pltpu
from jax.sharding import PartitionSpec as P


AXES = ("rep", "shard")
DEPTH = 4
LEFT_ROWS = 512
FINAL_ROWS = 128
F32, BF16 = jnp.float32, jnp.bfloat16
HIGHEST = lax.Precision.HIGHEST
NT = (((1,), (1,)), ((), ()))
NN = (((1,), (0,)), ((), ()))
TT = (((0,), (1,)), ((), ()))
VMEM = pl.BlockSpec(memory_space=pltpu.VMEM)
SMEM = pl.BlockSpec(memory_space=pltpu.SMEM)
ANY = pl.BlockSpec(memory_space=pl.ANY)


def dot(a, b, dims, precision=None):
    return lax.dot_general(a, b, dims, precision=precision, preferred_element_type=F32)


def split(x):
    high = x.astype(BF16)
    return high, (x - high.astype(F32)).astype(BF16)


def params(mib):
    return pltpu.CompilerParams(vmem_limit_bytes=mib << 20)


def bit(code, index):
    return (code[0] >> index) & 1


def shape_of(*shape, dtype=F32):
    return jax.ShapeDtypeStruct(shape, dtype)


def left_kernel(block, jobs, code, grad, error, basis, *refs):
    outs, (grads, errors, factors, sems) = refs[:-4], refs[-4:]
    rank = basis.shape[1]
    copies = [pltpu.make_async_copy(basis, factors, sems.at[2, 0])]
    copies[0].start()
    blocks = []
    for job, (which, begin, end) in enumerate(jobs):
        w = bit(code, which)
        for start in range(begin, end, block):
            i = len(blocks)
            source, target = pl.ds(start, block), pl.ds(i * block, block)
            pair = (
                pltpu.make_async_copy(error.at[0, w, source], errors.at[target], sems.at[0, i]),
                pltpu.make_async_copy(grad.at[0, w, source], grads.at[target], sems.at[1, i]),
            )
            blocks.append((job, start, pair))

    def begin_block(i):
        if i < len(blocks):
            for copy in blocks[i][2]:
                copy.start()

    for i in range(DEPTH):
        begin_block(i)
    copies[0].wait()
    cuts = []
    for which, _, _ in jobs:
        top, rest = split(factors[bit(code, which)])
        cuts.append((top, jnp.concatenate([top, rest], axis=0)))
    for i, (job, start, pair) in enumerate(blocks):
        for copy in pair:
            copy.wait()
        begin_block(i + DEPTH)
        top, cut = cuts[job]
        high, low, left = outs[3 * job : 3 * job + 3]
        source, target = slice(start, start + block), slice(i * block, (i + 1) * block)
        upper, lower = split(grads[target].astype(F32) + errors[target])
        high[source] = upper
        low[source] = lower
        both = dot(cut, upper, NT)
        left[:, source] = both[:rank] + both[rank:] + dot(top, lower, NT)


def left_of(jobs, code, grad, error, basis):
    _, _, rows, cols = grad.shape
    rank = basis.shape[1]
    block = min(rows, LEFT_ROWS)
    total = sum(end - begin for _, begin, end in jobs)
    return pl.pallas_call(
        functools.partial(left_kernel, block, jobs),
        name="left",
        in_specs=[SMEM, ANY, ANY, ANY],
        out_specs=[VMEM] * (3 * len(jobs)),
        out_shape=[
            shape_of(rows, cols, dtype=BF16),
            shape_of(rows, cols, dtype=BF16),
            shape_of(rank, rows),
        ]
        * len(jobs),
        scratch_shapes=[
            pltpu.VMEM((total, cols), BF16),
            pltpu.VMEM((total, cols), F32),
            pltpu.VMEM(basis.shape, F32),
            pltpu.SemaphoreType.DMA((3, total // block)),
        ],
        compiler_params=params(24),
        cost_estimate=pl.CostEstimate(
            flops=6 * total * cols * rank, bytes_accessed=10 * total * cols, transcendentals=0
        ),
    )(code, grad, error, basis)


def ordered(left, keep):
    half = left.shape[0] // 2
    pick = lambda index: left[pl.ds(pl.multiple_of(index * half, half), half), :]
    return jnp.concatenate([pick(1 - keep), pick(keep)], axis=0)


def product(left, high, low, columns):
    rank = left.shape[0]
    top, rest = split(left)
    both = dot(jnp.concatenate([top, rest], axis=0), high[:, columns], NN)
    return both[:rank] + both[rank:] + dot(top, low[:, columns], NN)


def right_kernel(starts, keeps, with_gram, code, left, high, low, *outs):
    for start, keep, right in zip(starts, keeps, outs):
        columns = slice(start, start + right.shape[1])
        chosen = left[...] if keep is None else ordered(left, bit(code, keep))
        right[...] = product(chosen, high, low, columns)
    if with_gram:
        half = left.shape[0] // 2
        gram = dot(left[...], left[...], NT, HIGHEST)
        outs[-1][...] = jnp.concatenate([gram[:half], gram[half:]], axis=1)


def right_of(columns, keeps, code, left, high, low, with_gram=False):
    rows, _ = high.shape
    rank = left.shape[0]
    width = sum(width for _, width in columns)
    out_shape = [shape_of(rank, width) for _, width in columns]
    if with_gram:
        out_shape.append(shape_of(rank // 2, 2 * rank))
    return pl.pallas_call(
        functools.partial(right_kernel, [start for start, _ in columns], keeps, with_gram),
        name="right",
        in_specs=[SMEM] + [VMEM] * 3,
        out_specs=[VMEM] * len(out_shape),
        out_shape=out_shape,
        compiler_params=params(8),
        cost_estimate=pl.CostEstimate(
            flops=6 * rows * width * rank, bytes_accessed=4 * rows * width, transcendentals=0
        ),
    )(code, left, high, low)


def eliminate(whole, begin, end):
    rank = whole.shape[0]
    tile = 8
    work = [whole[i : i + tile] for i in range(0, rank, tile)]
    inside = lax.broadcasted_iota(jnp.int32, (tile, 1), 0)
    spread = lambda array: jnp.broadcast_to(array, (tile, 2 * rank))
    for j in range(begin, end, 2):
        home, at = divmod(j, tile)
        first, second = spread(work[home][at : at + 1]), spread(work[home][at + 1 : at + 2])
        a, b = spread(first[:, j : j + 1]), spread(first[:, j + 1 : j + 2])
        c = spread(second[:, j + 1 : j + 2])
        over = 1.0 / (a * c - b * b)
        one = (c * first - b * second) * over
        two = (a * second - b * first) * over
        for k in range(home, rank // tile):
            x, y = spread(work[k][:, j : j + 1]), spread(work[k][:, j + 1 : j + 2])
            if k == home:
                x = jnp.where(inside > at + 1, x, 0.0)
                y = jnp.where(inside > at + 1, y, 0.0)
            work[k] = work[k] - x * one - y * two
    return jnp.concatenate(work, axis=0)


def opening_kernel(end, packed, out):
    rank = out.shape[0]
    sums = packed[:, packed.shape[1] - 2 * rank :]
    row = lax.broadcasted_iota(jnp.int32, (rank, rank), 0)
    col = lax.broadcasted_iota(jnp.int32, (rank, rank), 1)
    gram = jnp.concatenate([sums[:, :rank], sums[:, rank:]], axis=0)
    whole = jnp.concatenate([gram, jnp.where(row == col, 1.0, 0.0)], axis=1)
    out[...] = eliminate(whole, 0, end)


def closing_kernel(begin, work, inverse):
    rank = inverse.shape[0]
    row = lax.broadcasted_iota(jnp.int32, (rank, 2 * rank), 0)
    col = lax.broadcasted_iota(jnp.int32, (rank, 2 * rank), 1)
    whole = eliminate(work[...], begin, rank - 2)
    above = jnp.concatenate([whole[-1:], whole[:-1]], axis=0)
    before = col == row - 1
    pick = lambda array, mask: jnp.sum(jnp.where(mask, array, 0.0), axis=1, keepdims=True)
    odd = row[:, :1] % 2 == 1
    pivot = jnp.where(odd, pick(above, before), 1.0)
    ratio = jnp.where(odd, pick(whole, before) / pivot, 0.0)
    whole = whole - ratio * above
    inverse[...] = whole[:, rank:] / jnp.sqrt(pick(whole, col == row))


def factor_of(kernel, array, rank, width):
    return pl.pallas_call(
        kernel,
        name="factor",
        in_specs=[VMEM],
        out_specs=VMEM,
        out_shape=shape_of(rank, width),
        compiler_params=params(8),
        cost_estimate=pl.CostEstimate(
            flops=2 * rank**3, bytes_accessed=8 * rank * rank, transcendentals=rank
        ),
    )(array)


def final_kernel(block, scale, keeps, code, *refs):
    update, new_error, basis_next, updates, errors, rights, sems = refs[-7:]
    count = (len(refs) - 7) // 2
    copies = []
    for which in range(2):
        inverse, left, high, low, *totals = refs[count * which : count * (which + 1)]
        rows = left.shape[1]
        w = bit(code, which)
        start = 0
        pieces = []
        for keep, total in zip(keeps, totals):
            columns = slice(start, start + total.shape[1])
            right = dot(inverse[...], ordered(total, 1 - bit(code, keep)) * scale, NN, HIGHEST)
            rights[which, :, columns] = right
            top, rest = split(right)
            pieces.append(jnp.concatenate([top, rest, top], axis=0))
            start += total.shape[1]
        pieces = jnp.concatenate(pieces, axis=1)
        copies.append(pltpu.make_async_copy(rights.at[which], basis_next.at[w], sems.at[which, 2, 0]))
        copies[-1].start()
        top, rest = split(dot(left[...], inverse[...], TT, HIGHEST))
        ortho = jnp.concatenate([top, top, rest], axis=1)
        for i, start in enumerate(range(0, rows, block)):
            part, where = slice(start, start + block), pl.ds(start, block)
            approx = dot(ortho[part], pieces, NN)
            updates[which, part] = approx.astype(BF16)
            errors[which, part] = (high[part].astype(F32) + low[part].astype(F32)) - approx
            for kind, source, target in (
                (0, errors.at[which, where], new_error.at[0, w, where]),
                (1, updates.at[which, where], update.at[w, where]),
            ):
                copies.append(pltpu.make_async_copy(source, target, sems.at[which, kind, i]))
                copies[-1].start()
    for copy in copies:
        copy.wait()


def final_of(keeps, code, mine, theirs, scale):
    rank, rows = mine[1].shape
    cols = mine[2].shape[1]
    block = min(rows, FINAL_ROWS)
    return pl.pallas_call(
        functools.partial(final_kernel, block, scale, keeps),
        name="final",
        in_specs=[SMEM] + [VMEM] * (2 * len(mine)),
        out_specs=[ANY] * 3,
        out_shape=[
            shape_of(2, rows, cols, dtype=BF16),
            shape_of(1, 2, rows, cols),
            shape_of(2, rank, cols),
        ],
        scratch_shapes=[
            pltpu.VMEM((2, rows, cols), BF16),
            pltpu.VMEM((2, rows, cols), F32),
            pltpu.VMEM((2, rank, cols), F32),
            pltpu.SemaphoreType.DMA((2, 3, rows // block)),
        ],
        compiler_params=params(24),
        cost_estimate=pl.CostEstimate(
            flops=12 * rows * cols * rank, bytes_accessed=20 * rows * cols, transcendentals=0
        ),
    )(code, *mine, *theirs)


def bits_of(count):
    return [1 << k for k in range(count.bit_length() - 1)]


def plan(replicas, shards):
    r = [(mask, 0) for mask in bits_of(replicas)[1:]]
    t = [(0, mask) for mask in bits_of(shards)]
    orders = (t + r, r + t)
    return r, t, orders


def on_device(replicas, shards, grad_kv, error_kv, basis_kv):
    def swap(value, masks):
        pairs = [
            (i * shards + j, (i ^ masks[0]) * shards + (j ^ masks[1]))
            for i in range(replicas)
            for j in range(shards)
        ]
        return lax.ppermute(value, AXES, pairs)

    def core(value):
        return swap(value, (1, 0))

    r, t, orders = plan(replicas, shards)
    scale = 1.0 / replicas

    rep, shard = lax.axis_index("rep"), lax.axis_index("shard")
    side = rep & 1
    code = side + 2 * (1 - side)
    for part, order in enumerate(orders):
        kept = ((rep & order[0][0]) + (shard & order[0][1]) > 0).astype(jnp.int32)
        code += kept << (2 + part)
    code = code.astype(jnp.int32).reshape(1)
    mine, theirs = 0, 1
    keeps = (2, 3)

    basis = basis_kv.transpose(0, 2, 1)
    grad_kv, error_kv, basis = (
        pltpu.with_memory_space_constraint(x, pltpu.HBM) for x in (grad_kv, error_kv, basis)
    )
    rank = basis.shape[1]
    rows, cols = grad_kv.shape[2:]

    jobs = (theirs, 0, rows), (mine, 0, rows)
    high_t, low_t, left_t, high_m, low_m, left_m = left_of(jobs, code, grad_kv, error_kv, basis)
    arriving = core(left_t)
    left_m = left_m + arriving
    for step in r:
        left_m = left_m + swap(left_m, step)
    left_m = left_m * scale
    left_t = core(left_m)

    first = cols * 3 // 8
    columns = ((0, first), (first, cols - first))
    *rights, gram = right_of(columns, keeps, code, left_m, high_m, low_m, True)
    arrivals = [
        core(right_of((columns[part],), (keeps[part],), code, left_t, high_t, low_t)[0])
        for part in range(2)
    ]
    totals_m, totals_t = [], []
    for part, (_, width) in enumerate(columns):
        right = rights[part] + arrivals[part]
        send, stay = right[: rank // 2], right[rank // 2 :]
        if part == 0:
            send, stay = (jnp.concatenate([x, gram], axis=1) for x in (send, stay))
        steps = orders[part]
        for turn, step in enumerate(steps):
            if part == 0 and turn == len(t):
                work = factor_of(functools.partial(opening_kernel, rank // 2), stay, rank, 2 * rank)
                inverse_m = factor_of(functools.partial(closing_kernel, rank // 2), work, rank, rank)
                stay = stay[:, :width]
            arrived = swap(send if turn == 0 else stay, step)
            stay = stay + arrived
        back = swap(stay, steps[0])
        total = jnp.concatenate([stay, back], axis=0)
        totals_m.append(total)
        totals_t.append(core(total))
    inverse_t = core(inverse_m)

    update, new_error, right = final_of(
        keeps,
        code,
        (inverse_m, left_m, high_m, low_m, *totals_m),
        (inverse_t, left_t, high_t, low_t, *totals_t),
        scale,
    )
    return update, new_error, right.transpose(0, 2, 1)


def solution(mesh):
    replicas, shards = mesh.shape["rep"], mesh.shape["shard"]
    placed = (P("rep", None, "shard", None), P("rep", None, "shard", None), P())

    def body(*args):
        return on_device(replicas, shards, *args)

    step = jax.shard_map(
        body,
        mesh=mesh,
        in_specs=placed,
        out_specs=(P(None, "shard", None), P("rep", None, "shard", None), P()),
        check_vma=False,
    )
    _, _, _ = plan(replicas, shards)
    return step
```

```python
import functools

import jax
import jax.numpy as jnp
from jax import lax
from jax.experimental import pallas as pl
from jax.experimental.pallas import tpu as pltpu
from jax.sharding import PartitionSpec as P


AXES = ("rep", "shard")
DEPTH = 4
LEFT_ROWS = 512
FINAL_ROWS = 128
F32, BF16 = jnp.float32, jnp.bfloat16
HIGHEST = lax.Precision.HIGHEST
NT = (((1,), (1,)), ((), ()))
NN = (((1,), (0,)), ((), ()))
TT = (((0,), (1,)), ((), ()))
VMEM = pl.BlockSpec(memory_space=pltpu.VMEM)
SMEM = pl.BlockSpec(memory_space=pltpu.SMEM)
ANY = pl.BlockSpec(memory_space=pl.ANY)


def dot(a, b, dims, precision=None):
    return lax.dot_general(a, b, dims, precision=precision, preferred_element_type=F32)


def split(x):
    high = x.astype(BF16)
    return high, (x - high.astype(F32)).astype(BF16)


def params(mib):
    return pltpu.CompilerParams(vmem_limit_bytes=mib << 20)


def bit(code, index):
    return (code[0] >> index) & 1


def shape_of(*shape, dtype=F32):
    return jax.ShapeDtypeStruct(shape, dtype)


def left_kernel(block, jobs, code, grad, error, basis, *refs):
    outs, (grads, errors, factors, sems) = refs[:-4], refs[-4:]
    rank = basis.shape[1]
    copies = [pltpu.make_async_copy(basis, factors, sems.at[2, 0])]
    copies[0].start()
    blocks = []
    for job, (which, begin, end) in enumerate(jobs):
        w = bit(code, which)
        for start in range(begin, end, block):
            i = len(blocks)
            source, target = pl.ds(start, block), pl.ds(i * block, block)
            pair = (
                pltpu.make_async_copy(error.at[0, w, source], errors.at[target], sems.at[0, i]),
                pltpu.make_async_copy(grad.at[0, w, source], grads.at[target], sems.at[1, i]),
            )
            blocks.append((job, start, pair))

    def begin_block(i):
        if i < len(blocks):
            for copy in blocks[i][2]:
                copy.start()

    for i in range(DEPTH):
        begin_block(i)
    copies[0].wait()
    cuts = []
    for which, _, _ in jobs:
        top, rest = split(factors[bit(code, which)])
        cuts.append((top, jnp.concatenate([top, rest], axis=0)))
    for i, (job, start, pair) in enumerate(blocks):
        for copy in pair:
            copy.wait()
        begin_block(i + DEPTH)
        top, cut = cuts[job]
        high, low, left = outs[3 * job : 3 * job + 3]
        source, target = slice(start, start + block), slice(i * block, (i + 1) * block)
        upper, lower = split(grads[target].astype(F32) + errors[target])
        high[source] = upper
        low[source] = lower
        both = dot(cut, upper, NT)
        left[:, source] = both[:rank] + both[rank:] + dot(top, lower, NT)


def left_of(jobs, code, grad, error, basis):
    _, _, rows, cols = grad.shape
    rank = basis.shape[1]
    block = min(rows, LEFT_ROWS)
    total = sum(end - begin for _, begin, end in jobs)
    return pl.pallas_call(
        functools.partial(left_kernel, block, jobs),
        name="left",
        in_specs=[SMEM, ANY, ANY, ANY],
        out_specs=[VMEM] * (3 * len(jobs)),
        out_shape=[
            shape_of(rows, cols, dtype=BF16),
            shape_of(rows, cols, dtype=BF16),
            shape_of(rank, rows),
        ]
        * len(jobs),
        scratch_shapes=[
            pltpu.VMEM((total, cols), BF16),
            pltpu.VMEM((total, cols), F32),
            pltpu.VMEM(basis.shape, F32),
            pltpu.SemaphoreType.DMA((3, total // block)),
        ],
        compiler_params=params(24),
        cost_estimate=pl.CostEstimate(
            flops=6 * total * cols * rank, bytes_accessed=10 * total * cols, transcendentals=0
        ),
    )(code, grad, error, basis)


def ordered(left, keep):
    half = left.shape[0] // 2
    pick = lambda index: left[pl.ds(pl.multiple_of(index * half, half), half), :]
    return jnp.concatenate([pick(1 - keep), pick(keep)], axis=0)


def product(left, high, low, columns):
    rank = left.shape[0]
    top, rest = split(left)
    both = dot(jnp.concatenate([top, rest], axis=0), high[:, columns], NN)
    return both[:rank] + both[rank:] + dot(top, low[:, columns], NN)


def right_kernel(starts, keeps, with_gram, code, left, high, low, *outs):
    for start, keep, right in zip(starts, keeps, outs):
        columns = slice(start, start + right.shape[1])
        chosen = left[...] if keep is None else ordered(left, bit(code, keep))
        right[...] = product(chosen, high, low, columns)
    if with_gram:
        half = left.shape[0] // 2
        gram = dot(left[...], left[...], NT, HIGHEST)
        outs[-1][...] = jnp.concatenate([gram[:half], gram[half:]], axis=1)


def right_of(columns, keeps, code, left, high, low, with_gram=False):
    rows, _ = high.shape
    rank = left.shape[0]
    width = sum(width for _, width in columns)
    out_shape = [shape_of(rank, width) for _, width in columns]
    if with_gram:
        out_shape.append(shape_of(rank // 2, 2 * rank))
    return pl.pallas_call(
        functools.partial(right_kernel, [start for start, _ in columns], keeps, with_gram),
        name="right",
        in_specs=[SMEM] + [VMEM] * 3,
        out_specs=[VMEM] * len(out_shape),
        out_shape=out_shape,
        compiler_params=params(8),
        cost_estimate=pl.CostEstimate(
            flops=6 * rows * width * rank, bytes_accessed=4 * rows * width, transcendentals=0
        ),
    )(code, left, high, low)


def eliminate(whole, begin, end):
    rank = whole.shape[0]
    tile = 8
    work = [whole[i : i + tile] for i in range(0, rank, tile)]
    inside = lax.broadcasted_iota(jnp.int32, (tile, 1), 0)
    spread = lambda array: jnp.broadcast_to(array, (tile, 2 * rank))
    for j in range(begin, end, 2):
        home, at = divmod(j, tile)
        first, second = spread(work[home][at : at + 1]), spread(work[home][at + 1 : at + 2])
        a, b = spread(first[:, j : j + 1]), spread(first[:, j + 1 : j + 2])
        c = spread(second[:, j + 1 : j + 2])
        over = 1.0 / (a * c - b * b)
        one = (c * first - b * second) * over
        two = (a * second - b * first) * over
        for k in range(home, rank // tile):
            x, y = spread(work[k][:, j : j + 1]), spread(work[k][:, j + 1 : j + 2])
            if k == home:
                x = jnp.where(inside > at + 1, x, 0.0)
                y = jnp.where(inside > at + 1, y, 0.0)
            work[k] = work[k] - x * one - y * two
    return jnp.concatenate(work, axis=0)


def opening_kernel(end, packed, out):
    rank = out.shape[0]
    sums = packed[:, packed.shape[1] - 2 * rank :]
    row = lax.broadcasted_iota(jnp.int32, (rank, rank), 0)
    col = lax.broadcasted_iota(jnp.int32, (rank, rank), 1)
    gram = jnp.concatenate([sums[:, :rank], sums[:, rank:]], axis=0)
    whole = jnp.concatenate([gram, jnp.where(row == col, 1.0, 0.0)], axis=1)
    out[...] = eliminate(whole, 0, end)


def closing_kernel(begin, work, inverse):
    rank = inverse.shape[0]
    row = lax.broadcasted_iota(jnp.int32, (rank, 2 * rank), 0)
    col = lax.broadcasted_iota(jnp.int32, (rank, 2 * rank), 1)
    whole = eliminate(work[...], begin, rank - 2)
    above = jnp.concatenate([whole[-1:], whole[:-1]], axis=0)
    before = col == row - 1
    pick = lambda array, mask: jnp.sum(jnp.where(mask, array, 0.0), axis=1, keepdims=True)
    odd = row[:, :1] % 2 == 1
    pivot = jnp.where(odd, pick(above, before), 1.0)
    ratio = jnp.where(odd, pick(whole, before) / pivot, 0.0)
    whole = whole - ratio * above
    inverse[...] = whole[:, rank:] / jnp.sqrt(pick(whole, col == row))


def factor_of(kernel, array, rank, width):
    return pl.pallas_call(
        kernel,
        name="factor",
        in_specs=[VMEM],
        out_specs=VMEM,
        out_shape=shape_of(rank, width),
        compiler_params=params(8),
        cost_estimate=pl.CostEstimate(
            flops=2 * rank**3, bytes_accessed=8 * rank * rank, transcendentals=rank
        ),
    )(array)


def prepare(code, keeps, scale, inverse, left, totals):
    rights = [
        dot(inverse[...], ordered(total, 1 - bit(code, keep)) * scale, NN, HIGHEST)
        for keep, total in zip(keeps, totals)
    ]
    right = jnp.concatenate(rights, axis=1)
    top, rest = split(right)
    pieces = jnp.concatenate([top, rest, top], axis=0)
    top, rest = split(dot(left[...], inverse[...], TT, HIGHEST))
    return right, pieces, jnp.concatenate([top, top, rest], axis=1)


def prepare_kernel(keeps, scale, code, inverse, left, *refs):
    outs = prepare(code, keeps, scale, inverse, left, refs[:-3])
    for ref, value in zip(refs[-3:], outs):
        ref[...] = value


def prepare_of(keeps, code, scale, inverse, left, *totals):
    rank, rows = left.shape
    cols = sum(total.shape[1] for total in totals)
    return pl.pallas_call(
        functools.partial(prepare_kernel, keeps, scale),
        name="prepare",
        in_specs=[SMEM] + [VMEM] * (2 + len(totals)),
        out_specs=[VMEM] * 3,
        out_shape=[
            shape_of(rank, cols),
            shape_of(3 * rank, cols, dtype=BF16),
            shape_of(rows, 3 * rank, dtype=BF16),
        ],
        compiler_params=params(8),
        cost_estimate=pl.CostEstimate(
            flops=24 * rank * rank * cols, bytes_accessed=20 * rank * cols, transcendentals=0
        ),
    )(code, inverse, left, *totals)


def final_kernel(block, scale, keeps, code, *refs):
    update, new_error, basis_next, updates, errors, rights, sems = refs[-7:]
    right_m, pieces_m, ortho_m, high_m, low_m, inverse_t, left_t, high_t, low_t, *totals_t = refs[:-7]
    rows = high_m.shape[0]
    copies = []

    def send(which, kind, i, source, target):
        copies.append(pltpu.make_async_copy(source, target, sems.at[which, kind, i]))
        copies[-1].start()

    for which in range(2):
        w = bit(code, which)
        if which == 0:
            pieces, ortho, high, low = pieces_m[...], ortho_m, high_m, low_m
            send(which, 2, 0, right_m, basis_next.at[w])
        else:
            right, pieces, ortho = prepare(code, keeps, scale, inverse_t, left_t, totals_t)
            high, low = high_t, low_t
            rights[...] = right
            send(which, 2, 0, rights, basis_next.at[w])
        for i, start in enumerate(range(0, rows, block)):
            part, where = slice(start, start + block), pl.ds(start, block)
            approx = dot(ortho[part], pieces, NN)
            updates[which, part] = approx.astype(BF16)
            errors[which, part] = (high[part].astype(F32) + low[part].astype(F32)) - approx
            send(which, 0, i, errors.at[which, where], new_error.at[0, w, where])
            send(which, 1, i, updates.at[which, where], update.at[w, where])
    for copy in copies:
        copy.wait()


def final_of(keeps, code, mine, theirs, scale):
    rank = mine[0].shape[0]
    rows, cols = mine[3].shape
    block = min(rows, FINAL_ROWS)
    return pl.pallas_call(
        functools.partial(final_kernel, block, scale, keeps),
        name="final",
        in_specs=[SMEM] + [VMEM] * (len(mine) + len(theirs)),
        out_specs=[ANY] * 3,
        out_shape=[
            shape_of(2, rows, cols, dtype=BF16),
            shape_of(1, 2, rows, cols),
            shape_of(2, rank, cols),
        ],
        scratch_shapes=[
            pltpu.VMEM((2, rows, cols), BF16),
            pltpu.VMEM((2, rows, cols), F32),
            pltpu.VMEM((rank, cols), F32),
            pltpu.SemaphoreType.DMA((2, 3, rows // block)),
        ],
        compiler_params=params(24),
        cost_estimate=pl.CostEstimate(
            flops=12 * rows * cols * rank, bytes_accessed=20 * rows * cols, transcendentals=0
        ),
    )(code, *mine, *theirs)


def bits_of(count):
    return [1 << k for k in range(count.bit_length() - 1)]


def plan(replicas, shards):
    r = [(mask, 0) for mask in bits_of(replicas)[1:]]
    t = [(0, mask) for mask in bits_of(shards)]
    orders = (t + r, r + t)
    return r, t, orders


def on_device(replicas, shards, grad_kv, error_kv, basis_kv):
    def swap(value, masks):
        pairs = [
            (i * shards + j, (i ^ masks[0]) * shards + (j ^ masks[1]))
            for i in range(replicas)
            for j in range(shards)
        ]
        return lax.ppermute(value, AXES, pairs)

    def core(value):
        return swap(value, (1, 0))

    r, t, orders = plan(replicas, shards)
    scale = 1.0 / replicas

    rep, shard = lax.axis_index("rep"), lax.axis_index("shard")
    side = rep & 1
    code = side + 2 * (1 - side)
    for part, order in enumerate(orders):
        kept = ((rep & order[0][0]) + (shard & order[0][1]) > 0).astype(jnp.int32)
        code += kept << (2 + part)
    code = code.astype(jnp.int32).reshape(1)
    mine, theirs = 0, 1
    keeps = (2, 3)

    basis = basis_kv.transpose(0, 2, 1)
    grad_kv, error_kv, basis = (
        pltpu.with_memory_space_constraint(x, pltpu.HBM) for x in (grad_kv, error_kv, basis)
    )
    rank = basis.shape[1]
    rows, cols = grad_kv.shape[2:]

    jobs = (theirs, 0, rows), (mine, 0, rows)
    high_t, low_t, left_t, high_m, low_m, left_m = left_of(jobs, code, grad_kv, error_kv, basis)
    arriving = core(left_t)
    left_m = left_m + arriving
    for step in r:
        left_m = left_m + swap(left_m, step)
    left_m = left_m * scale
    left_t = core(left_m)

    first = cols * 3 // 8
    columns = ((0, first), (first, cols - first))
    *rights, gram = right_of(columns, keeps, code, left_m, high_m, low_m, True)
    arrivals = [
        core(right_of((columns[part],), (keeps[part],), code, left_t, high_t, low_t)[0])
        for part in range(2)
    ]
    totals_m, totals_t = [], []
    for part, (_, width) in enumerate(columns):
        right = rights[part] + arrivals[part]
        send, stay = right[: rank // 2], right[rank // 2 :]
        if part == 0:
            send, stay = (jnp.concatenate([x, gram], axis=1) for x in (send, stay))
        steps = orders[part]
        for turn, step in enumerate(steps):
            if part == 0 and turn == len(t):
                work = factor_of(functools.partial(opening_kernel, rank // 2), stay, rank, 2 * rank)
                inverse_m = factor_of(functools.partial(closing_kernel, rank // 2), work, rank, rank)
                stay = stay[:, :width]
            arrived = swap(send if turn == 0 else stay, step)
            stay = stay + arrived
        back = swap(stay, steps[0])
        total = jnp.concatenate([stay, back], axis=0)
        totals_m.append(total)
        totals_t.append(core(total))
        if part == 0:
            inverse_t = core(inverse_m)

    ready = prepare_of(keeps, code, scale, inverse_m, left_m, *totals_m)
    update, new_error, right = final_of(
        keeps,
        code,
        (*ready, high_m, low_m),
        (inverse_t, left_t, high_t, low_t, *totals_t),
        scale,
    )
    return update, new_error, right.transpose(0, 2, 1)


def solution(mesh):
    replicas, shards = mesh.shape["rep"], mesh.shape["shard"]
    placed = (P("rep", None, "shard", None), P("rep", None, "shard", None), P())

    def body(*args):
        return on_device(replicas, shards, *args)

    step = jax.shard_map(
        body,
        mesh=mesh,
        in_specs=placed,
        out_specs=(P(None, "shard", None), P("rep", None, "shard", None), P()),
        check_vma=False,
    )
    _, _, _ = plan(replicas, shards)
    return step
```

```python
import functools

import jax
import jax.numpy as jnp
from jax import lax
from jax.experimental import pallas as pl
from jax.experimental.pallas import tpu as pltpu
from jax.sharding import PartitionSpec as P


AXES = ("rep", "shard")
DEPTH = 4
LEFT_ROWS = 512
FINAL_ROWS = 128
F32, BF16 = jnp.float32, jnp.bfloat16
HIGHEST = lax.Precision.HIGHEST
NT = (((1,), (1,)), ((), ()))
NN = (((1,), (0,)), ((), ()))
TT = (((0,), (1,)), ((), ()))
VMEM = pl.BlockSpec(memory_space=pltpu.VMEM)
SMEM = pl.BlockSpec(memory_space=pltpu.SMEM)
ANY = pl.BlockSpec(memory_space=pl.ANY)


def dot(a, b, dims, precision=None):
    return lax.dot_general(a, b, dims, precision=precision, preferred_element_type=F32)


def split(x):
    high = x.astype(BF16)
    return high, (x - high.astype(F32)).astype(BF16)


def params(mib):
    return pltpu.CompilerParams(vmem_limit_bytes=mib << 20)


def bit(code, index):
    return (code[0] >> index) & 1


def shape_of(*shape, dtype=F32):
    return jax.ShapeDtypeStruct(shape, dtype)


def left_kernel(block, jobs, code, grad, error, basis, *refs):
    *outs, late_error, late_grad, late_basis = refs[:-4]
    grads, errors, factors, sems = refs[-4:]
    rank = basis.shape[1]
    copies = [pltpu.make_async_copy(basis, factors, sems.at[2, 0])]
    copies[0].start()
    blocks = []
    for job, (which, begin, end) in enumerate(jobs):
        w = bit(code, which)
        for start in range(begin, end, block):
            i = len(blocks)
            source, target = pl.ds(start, block), pl.ds(i * block, block)
            pair = (
                pltpu.make_async_copy(error.at[0, w, source], errors.at[target], sems.at[0, i]),
                pltpu.make_async_copy(grad.at[0, w, source], grads.at[target], sems.at[1, i]),
            )
            blocks.append((job, start, pair))

    def begin_block(i):
        if i < len(blocks):
            for copy in blocks[i][2]:
                copy.start()

    for i in range(DEPTH):
        begin_block(i)
    which, _, end = jobs[-1]
    w, i, rest = bit(code, which), len(blocks), pl.ds(end, late_grad.shape[0])
    late = (
        pltpu.make_async_copy(error.at[0, w, rest], late_error, sems.at[0, i]),
        pltpu.make_async_copy(grad.at[0, w, rest], late_grad, sems.at[1, i]),
    )
    for copy in late:
        copy.start()
    copies[0].wait()
    late_basis[...] = factors[w]
    cuts = []
    for which, _, _ in jobs:
        top, rest = split(factors[bit(code, which)])
        cuts.append((top, jnp.concatenate([top, rest], axis=0)))
    for i, (job, start, pair) in enumerate(blocks):
        for copy in pair:
            copy.wait()
        begin_block(i + DEPTH)
        top, cut = cuts[job]
        high, low, left = outs[3 * job : 3 * job + 3]
        source, target = slice(start, start + block), slice(i * block, (i + 1) * block)
        upper, lower = split(grads[target].astype(F32) + errors[target])
        high[source] = upper
        low[source] = lower
        both = dot(cut, upper, NT)
        left[:, source] = both[:rank] + both[rank:] + dot(top, lower, NT)
    for copy in late:
        copy.wait()


def late_kernel(begin, error, grad, basis, _high, _low, _left, high, low, left):
    rank, rows = left.shape
    part = slice(begin, rows)
    top, rest = split(basis[...])
    upper, lower = split(grad[...].astype(F32) + error[...])
    high[part] = upper
    low[part] = lower
    both = dot(jnp.concatenate([top, rest], axis=0), upper, NT)
    left[:, part] = both[:rank] + both[rank:] + dot(top, lower, NT)


def late_of(begin, error, grad, basis, high, low, left):
    rows, cols = high.shape
    rank = left.shape[0]
    return pl.pallas_call(
        functools.partial(late_kernel, begin),
        name="late",
        in_specs=[VMEM] * 6,
        out_specs=[VMEM] * 3,
        out_shape=[
            shape_of(rows, cols, dtype=BF16),
            shape_of(rows, cols, dtype=BF16),
            shape_of(rank, rows),
        ],
        input_output_aliases={3: 0, 4: 1, 5: 2},
        compiler_params=params(8),
        cost_estimate=pl.CostEstimate(
            flops=6 * (rows - begin) * cols * rank, bytes_accessed=8 * rows * cols, transcendentals=0
        ),
    )(error, grad, basis, high, low, left)


def left_of(jobs, code, grad, error, basis):
    _, _, rows, cols = grad.shape
    rank = basis.shape[1]
    block = min(rows // 2, LEFT_ROWS)
    late = rows - jobs[-1][2]
    total = sum(end - begin for _, begin, end in jobs)
    return pl.pallas_call(
        functools.partial(left_kernel, block, jobs),
        name="left",
        in_specs=[SMEM, ANY, ANY, ANY],
        out_specs=[VMEM] * (3 * len(jobs) + 3),
        out_shape=[
            shape_of(rows, cols, dtype=BF16),
            shape_of(rows, cols, dtype=BF16),
            shape_of(rank, rows),
        ]
        * len(jobs)
        + [shape_of(late, cols), shape_of(late, cols, dtype=BF16), shape_of(rank, cols)],
        scratch_shapes=[
            pltpu.VMEM((total, cols), BF16),
            pltpu.VMEM((total, cols), F32),
            pltpu.VMEM(basis.shape, F32),
            pltpu.SemaphoreType.DMA((3, total // block + 1)),
        ],
        compiler_params=params(24),
        cost_estimate=pl.CostEstimate(
            flops=6 * total * cols * rank, bytes_accessed=10 * total * cols, transcendentals=0
        ),
    )(code, grad, error, basis)


def ordered(left, keep):
    half = left.shape[0] // 2
    pick = lambda index: left[pl.ds(pl.multiple_of(index * half, half), half), :]
    return jnp.concatenate([pick(1 - keep), pick(keep)], axis=0)


def product(left, high, low, columns):
    rank = left.shape[0]
    top, rest = split(left)
    both = dot(jnp.concatenate([top, rest], axis=0), high[:, columns], NN)
    return both[:rank] + both[rank:] + dot(top, low[:, columns], NN)


def right_kernel(starts, keeps, with_gram, code, left, high, low, *outs):
    for start, keep, right in zip(starts, keeps, outs):
        columns = slice(start, start + right.shape[1])
        chosen = left[...] if keep is None else ordered(left, bit(code, keep))
        right[...] = product(chosen, high, low, columns)
    if with_gram:
        half = left.shape[0] // 2
        gram = dot(left[...], left[...], NT, HIGHEST)
        outs[-1][...] = jnp.concatenate([gram[:half], gram[half:]], axis=1)


def right_of(columns, keeps, code, left, high, low, with_gram=False):
    rows, _ = high.shape
    rank = left.shape[0]
    width = sum(width for _, width in columns)
    out_shape = [shape_of(rank, width) for _, width in columns]
    if with_gram:
        out_shape.append(shape_of(rank // 2, 2 * rank))
    return pl.pallas_call(
        functools.partial(right_kernel, [start for start, _ in columns], keeps, with_gram),
        name="right",
        in_specs=[SMEM] + [VMEM] * 3,
        out_specs=[VMEM] * len(out_shape),
        out_shape=out_shape,
        compiler_params=params(8),
        cost_estimate=pl.CostEstimate(
            flops=6 * rows * width * rank, bytes_accessed=4 * rows * width, transcendentals=0
        ),
    )(code, left, high, low)


def eliminate(whole, begin, end):
    rank = whole.shape[0]
    tile = 8
    work = [whole[i : i + tile] for i in range(0, rank, tile)]
    inside = lax.broadcasted_iota(jnp.int32, (tile, 1), 0)
    spread = lambda array: jnp.broadcast_to(array, (tile, 2 * rank))
    for j in range(begin, end, 2):
        home, at = divmod(j, tile)
        first, second = spread(work[home][at : at + 1]), spread(work[home][at + 1 : at + 2])
        a, b = spread(first[:, j : j + 1]), spread(first[:, j + 1 : j + 2])
        c = spread(second[:, j + 1 : j + 2])
        over = 1.0 / (a * c - b * b)
        one = (c * first - b * second) * over
        two = (a * second - b * first) * over
        for k in range(home, rank // tile):
            x, y = spread(work[k][:, j : j + 1]), spread(work[k][:, j + 1 : j + 2])
            if k == home:
                x = jnp.where(inside > at + 1, x, 0.0)
                y = jnp.where(inside > at + 1, y, 0.0)
            work[k] = work[k] - x * one - y * two
    return jnp.concatenate(work, axis=0)


def opening_kernel(end, packed, out):
    rank = out.shape[0]
    sums = packed[:, packed.shape[1] - 2 * rank :]
    row = lax.broadcasted_iota(jnp.int32, (rank, rank), 0)
    col = lax.broadcasted_iota(jnp.int32, (rank, rank), 1)
    gram = jnp.concatenate([sums[:, :rank], sums[:, rank:]], axis=0)
    whole = jnp.concatenate([gram, jnp.where(row == col, 1.0, 0.0)], axis=1)
    out[...] = eliminate(whole, 0, end)


def closing_kernel(begin, work, inverse):
    rank = inverse.shape[0]
    row = lax.broadcasted_iota(jnp.int32, (rank, 2 * rank), 0)
    col = lax.broadcasted_iota(jnp.int32, (rank, 2 * rank), 1)
    whole = eliminate(work[...], begin, rank - 2)
    above = jnp.concatenate([whole[-1:], whole[:-1]], axis=0)
    before = col == row - 1
    pick = lambda array, mask: jnp.sum(jnp.where(mask, array, 0.0), axis=1, keepdims=True)
    odd = row[:, :1] % 2 == 1
    pivot = jnp.where(odd, pick(above, before), 1.0)
    ratio = jnp.where(odd, pick(whole, before) / pivot, 0.0)
    whole = whole - ratio * above
    inverse[...] = whole[:, rank:] / jnp.sqrt(pick(whole, col == row))


def factor_of(kernel, array, rank, width):
    return pl.pallas_call(
        kernel,
        name="factor",
        in_specs=[VMEM],
        out_specs=VMEM,
        out_shape=shape_of(rank, width),
        compiler_params=params(8),
        cost_estimate=pl.CostEstimate(
            flops=2 * rank**3, bytes_accessed=8 * rank * rank, transcendentals=rank
        ),
    )(array)


def prepare(code, keeps, scale, inverse, left, totals):
    rights = [
        dot(inverse[...], ordered(total, 1 - bit(code, keep)) * scale, NN, HIGHEST)
        for keep, total in zip(keeps, totals)
    ]
    right = jnp.concatenate(rights, axis=1)
    top, rest = split(right)
    pieces = jnp.concatenate([top, rest, top], axis=0)
    top, rest = split(dot(left[...], inverse[...], TT, HIGHEST))
    return right, pieces, jnp.concatenate([top, top, rest], axis=1)


def prepare_kernel(keeps, scale, code, inverse, left, *refs):
    outs = prepare(code, keeps, scale, inverse, left, refs[:-3])
    for ref, value in zip(refs[-3:], outs):
        ref[...] = value


def prepare_of(keeps, code, scale, inverse, left, *totals):
    rank, rows = left.shape
    cols = sum(total.shape[1] for total in totals)
    return pl.pallas_call(
        functools.partial(prepare_kernel, keeps, scale),
        name="prepare",
        in_specs=[SMEM] + [VMEM] * (2 + len(totals)),
        out_specs=[VMEM] * 3,
        out_shape=[
            shape_of(rank, cols),
            shape_of(3 * rank, cols, dtype=BF16),
            shape_of(rows, 3 * rank, dtype=BF16),
        ],
        compiler_params=params(8),
        cost_estimate=pl.CostEstimate(
            flops=24 * rank * rank * cols, bytes_accessed=20 * rank * cols, transcendentals=0
        ),
    )(code, inverse, left, *totals)


def final_kernel(block, scale, keeps, code, *refs):
    update, new_error, basis_next, updates, errors, rights, sems = refs[-7:]
    right_m, pieces_m, ortho_m, high_m, low_m, inverse_t, left_t, high_t, low_t, *totals_t = refs[:-7]
    rows = high_m.shape[0]
    copies = []

    def send(which, kind, i, source, target):
        copies.append(pltpu.make_async_copy(source, target, sems.at[which, kind, i]))
        copies[-1].start()

    for which in range(2):
        w = bit(code, which)
        if which == 0:
            pieces, ortho, high, low = pieces_m[...], ortho_m, high_m, low_m
            send(which, 2, 0, right_m, basis_next.at[w])
        else:
            right, pieces, ortho = prepare(code, keeps, scale, inverse_t, left_t, totals_t)
            high, low = high_t, low_t
            rights[...] = right
            send(which, 2, 0, rights, basis_next.at[w])
        for i, start in enumerate(range(0, rows, block)):
            part, where = slice(start, start + block), pl.ds(start, block)
            approx = dot(ortho[part], pieces, NN)
            updates[which, part] = approx.astype(BF16)
            errors[which, part] = (high[part].astype(F32) + low[part].astype(F32)) - approx
            send(which, 0, i, errors.at[which, where], new_error.at[0, w, where])
            send(which, 1, i, updates.at[which, where], update.at[w, where])
    for copy in copies:
        copy.wait()


def final_of(keeps, code, mine, theirs, scale):
    rank = mine[0].shape[0]
    rows, cols = mine[3].shape
    block = min(rows, FINAL_ROWS)
    return pl.pallas_call(
        functools.partial(final_kernel, block, scale, keeps),
        name="final",
        in_specs=[SMEM] + [VMEM] * (len(mine) + len(theirs)),
        out_specs=[ANY] * 3,
        out_shape=[
            shape_of(2, rows, cols, dtype=BF16),
            shape_of(1, 2, rows, cols),
            shape_of(2, rank, cols),
        ],
        scratch_shapes=[
            pltpu.VMEM((2, rows, cols), BF16),
            pltpu.VMEM((2, rows, cols), F32),
            pltpu.VMEM((rank, cols), F32),
            pltpu.SemaphoreType.DMA((2, 3, rows // block)),
        ],
        compiler_params=params(24),
        cost_estimate=pl.CostEstimate(
            flops=12 * rows * cols * rank, bytes_accessed=20 * rows * cols, transcendentals=0
        ),
    )(code, *mine, *theirs)


def bits_of(count):
    return [1 << k for k in range(count.bit_length() - 1)]


def plan(replicas, shards):
    r = [(mask, 0) for mask in bits_of(replicas)[1:]]
    t = [(0, mask) for mask in bits_of(shards)]
    orders = (t + r, r + t)
    return r, t, orders


def on_device(replicas, shards, grad_kv, error_kv, basis_kv):
    def swap(value, masks):
        pairs = [
            (i * shards + j, (i ^ masks[0]) * shards + (j ^ masks[1]))
            for i in range(replicas)
            for j in range(shards)
        ]
        return lax.ppermute(value, AXES, pairs)

    def core(value):
        return swap(value, (1, 0))

    r, t, orders = plan(replicas, shards)
    scale = 1.0 / replicas

    rep, shard = lax.axis_index("rep"), lax.axis_index("shard")
    side = rep & 1
    code = side + 2 * (1 - side)
    for part, order in enumerate(orders):
        kept = ((rep & order[0][0]) + (shard & order[0][1]) > 0).astype(jnp.int32)
        code += kept << (2 + part)
    code = code.astype(jnp.int32).reshape(1)
    mine, theirs = 0, 1
    keeps = (2, 3)

    basis = basis_kv.transpose(0, 2, 1)
    grad_kv, error_kv, basis = (
        pltpu.with_memory_space_constraint(x, pltpu.HBM) for x in (grad_kv, error_kv, basis)
    )
    rank = basis.shape[1]
    rows, cols = grad_kv.shape[2:]

    ahead = rows // 2
    jobs = (theirs, 0, rows), (mine, 0, ahead)
    high_t, low_t, left_t, high_m, low_m, left_m, *late = left_of(
        jobs, code, grad_kv, error_kv, basis
    )
    arriving = core(left_t)
    high_m, low_m, left_m = late_of(ahead, *late, high_m, low_m, left_m)
    left_m = left_m + arriving
    for step in r:
        left_m = left_m + swap(left_m, step)
    left_m = left_m * scale
    left_t = core(left_m)

    first = cols * 3 // 8
    columns = ((0, first), (first, cols - first))
    *rights, gram = right_of(columns, keeps, code, left_m, high_m, low_m, True)
    arrivals = [
        core(right_of((columns[part],), (keeps[part],), code, left_t, high_t, low_t)[0])
        for part in range(2)
    ]
    totals_m, totals_t = [], []
    for part, (_, width) in enumerate(columns):
        right = rights[part] + arrivals[part]
        send, stay = right[: rank // 2], right[rank // 2 :]
        if part == 0:
            send, stay = (jnp.concatenate([x, gram], axis=1) for x in (send, stay))
        steps = orders[part]
        for turn, step in enumerate(steps):
            if part == 0 and turn == len(t):
                work = factor_of(functools.partial(opening_kernel, rank // 2), stay, rank, 2 * rank)
                inverse_m = factor_of(functools.partial(closing_kernel, rank // 2), work, rank, rank)
                stay = stay[:, :width]
            arrived = swap(send if turn == 0 else stay, step)
            stay = stay + arrived
        back = swap(stay, steps[0])
        total = jnp.concatenate([stay, back], axis=0)
        totals_m.append(total)
        totals_t.append(core(total))
        if part == 0:
            inverse_t = core(inverse_m)

    ready = prepare_of(keeps, code, scale, inverse_m, left_m, *totals_m)
    update, new_error, right = final_of(
        keeps,
        code,
        (*ready, high_m, low_m),
        (inverse_t, left_t, high_t, low_t, *totals_t),
        scale,
    )
    return update, new_error, right.transpose(0, 2, 1)


def solution(mesh):
    replicas, shards = mesh.shape["rep"], mesh.shape["shard"]
    placed = (P("rep", None, "shard", None), P("rep", None, "shard", None), P())

    def body(*args):
        return on_device(replicas, shards, *args)

    step = jax.shard_map(
        body,
        mesh=mesh,
        in_specs=placed,
        out_specs=(P(None, "shard", None), P("rep", None, "shard", None), P()),
        check_vma=False,
    )
    _, _, _ = plan(replicas, shards)
    return step
```
